32 devices in a mesh: groups: 2 (over y), chan: 4 (over z), seg: 2 (over x), freq: 2 (over core).
Axes of the slice: x: 2, y: 2, z: 4, core: 2. Of those that a mesh axis runs over, the one named last changes fastest.
Arguments:
- traces: bfloat16 [10, 1024, 4096], P('seg', ('groups', 'chan')), parts along dimension 1, may hold values from -120 to 120
- dead_mask: int32 [1024], P(('groups', 'chan')), parts along dimension 0, may hold values 0 or 1
- seg_counts: int32 [1024], P(('groups', 'chan')), parts along dimension 0, may hold values from 1 to 10
- offsets: int32 [4], replicated, may hold values from 1 to 128, as said below
Outputs:
- correlations: float32 [1024, 4, 512], P(('groups', 'chan', 'seg'), None, 'freq'), parts along dimension 0
The draws below stay inside these ranges and needn't reach their ends.
There are 2 independent parts, one for each index of `groups`. The reference program is written for one: setup_inputs(seed, part) draws one part's arguments, and reference() takes and returns one part's arrays. A program takes and returns all parts, laid end to end along the dimension named above; an argument that names none is the same for every part. Nothing has to cross between parts.
Inputs may be any that keep to these rules, and one draw needn't show every extreme that they name: The 4 offsets are distinct and one of them equals 128.
All inputs are finite; a program needn't handle non-finite values. No bound on the sum of `dead_mask` on one device may be relied on, other than what follows from the above.
Results may differ from the reference program's by a relative error of at most 0.0056.
Values may be sent and summed in bfloat16 or wider, within the bound.
A program may use at most 128 MiB of HBM per device.

```python
import math
import jax
import jax.numpy as jnp
from jax import lax

L = 4096
HALF = 32
LAGS = 512
K = 4
F = 2048
BAND = 128
C = 512
SEGS = 10


def draw_traces(key, part):
    gain_key, tap_key, noise_key = jax.random.split(key, 3)
    gains = jnp.exp(jax.random.uniform(gain_key, (1, C, 1), jnp.float32, 0.0, 2.302585))
    taps = jax.random.uniform(tap_key, (3, 1, C, 1), jnp.float32, -1.0, 1.0)
    tap_one = 0.9 * taps[0]
    tap_two = 0.6 * taps[1]
    tap_three = 0.3 * taps[2]
    noise = jnp.clip(jax.random.normal(noise_key, (SEGS, C, L + 3), jnp.float32), -4.0, 4.0)
    filtered = noise[:, :, 3:] + tap_one * noise[:, :, 2:-1] + tap_two * noise[:, :, 1:-2] + tap_three * noise[:, :, :-3]
    return (gains * filtered).astype(jnp.bfloat16)


def draw_offsets(key, part):
    chosen = jax.random.permutation(jax.random.fold_in(key, 11), BAND - 1)[:K - 1] + 1
    values = jnp.concatenate([chosen.astype(jnp.int32), jnp.full((1,), BAND, jnp.int32)])
    order = jax.random.permutation(jax.random.fold_in(key, 12), K)
    return values[order].astype(jnp.int32)


def place_ends(entries, rng, low, high):
    dims = entries.shape
    spot = [jax.random.randint(jax.random.fold_in(rng, axis), (), 0, dims[axis]) for axis in range(len(dims))]
    entries = entries.at[tuple(spot)].set(low)
    longest = dims.index(max(dims))
    spot[longest] = (spot[longest] + 1) % dims[longest]
    return entries.at[tuple(spot)].set(high)


def setup_inputs(seed: int = 0, part: int = 0) -> dict:
    streams_of = jax.random.split(jax.random.key(seed), 5)
    part_splits = jax.random.split(jax.random.fold_in(streams_of[4], part), 5)
    traces = draw_traces(jax.random.fold_in(jax.random.fold_in(streams_of[4], part), 71), part)
    dead_mask = place_ends((jax.random.randint(part_splits[1], (C,), 0, 8) < 7).astype(jnp.int32), jax.random.fold_in(part_splits[1], 1), 0, 1)
    seg_counts = place_ends(jax.random.randint(part_splits[2], (C,), 1, SEGS + 1), jax.random.fold_in(part_splits[2], 1), 1, SEGS).astype(jnp.int32)
    offsets = draw_offsets(jax.random.fold_in(streams_of[4], 71), part)
    return {"traces": traces, "dead_mask": dead_mask, "seg_counts": seg_counts, "offsets": offsets}


epsilon = 1e-06

def fourier_table(bin_first, bin_number, length):
    samples = jnp.arange(length, dtype=jnp.int32)[:, None]
    bin_index = bin_first + jnp.arange(bin_number, dtype=jnp.int32)[None, :]
    phases = (samples * bin_index % length).astype(jnp.float32) * (2.0 * math.pi / length)
    return jnp.concatenate([jnp.cos(phases), -jnp.sin(phases)], axis=1).astype(jnp.bfloat16)

def delay_table(bin_first, bin_number, length, lag_number, bin_total):
    bin_index = bin_first + jnp.arange(bin_number, dtype=jnp.int32)[:, None]
    shifts = jnp.arange(lag_number, dtype=jnp.int32)[None, :] - lag_number // 2
    phases = (bin_index * shifts % length).astype(jnp.float32) * (2.0 * math.pi / length)
    scaling = 1.0 / math.sqrt(bin_total)
    return jnp.concatenate([jnp.cos(phases) * scaling, -jnp.sin(phases) * scaling], axis=0)

def reference(traces, dead_mask, seg_counts, offsets):
    fourier = fourier_table(0, F, L).astype(jnp.float32)
    bin_index = jnp.arange(F, dtype=jnp.int32)
    window_count = (jnp.minimum(bin_index + HALF, F - 1) - jnp.maximum(bin_index - HALF, 0) + 1).astype(jnp.float32)
    alive = dead_mask.astype(jnp.float32)
    zero_rows = jnp.zeros((BAND, F), jnp.float32)

    def segment(stacked, inputs):
        samples, seg_number = inputs
        spectra = jnp.dot(samples.astype(jnp.float32), fourier, precision=lax.Precision.HIGHEST)
        real_part = spectra[:, :F]
        imag_part = spectra[:, F:]
        power_bins = real_part * real_part + imag_part * imag_part
        window_sum = lax.reduce_window(power_bins, jnp.zeros((), power_bins.dtype), lax.add, (1, 2 * HALF + 1), (1, 1), ((0, 0), (HALF, HALF)))
        valid_seg = alive * (seg_number < seg_counts).astype(jnp.float32)
        factor = valid_seg[:, None] / jnp.sqrt(window_sum / window_count + epsilon)
        white_re = real_part * factor
        white_im = imag_part * factor
        padded_re = jnp.concatenate([white_re, zero_rows], axis=0)
        padded_im = jnp.concatenate([white_im, zero_rows], axis=0)
        slots = []
        for slot in range(K):
            partner_re = lax.dynamic_slice_in_dim(padded_re, offsets[slot], C, 0)
            partner_im = lax.dynamic_slice_in_dim(padded_im, offsets[slot], C, 0)
            slots.append(jnp.concatenate([white_re * partner_re + white_im * partner_im, white_im * partner_re - white_re * partner_im], axis=1))
        return (stacked + jnp.stack(slots, axis=1), None)
    initial = jnp.zeros((C, K, 2 * F), jnp.float32)
    seg_numbers = jnp.arange(SEGS, dtype=jnp.int32)
    stacked, unused = lax.scan(segment, initial, (traces, seg_numbers))
    padded_counts = jnp.concatenate([seg_counts, jnp.zeros((BAND,), jnp.int32)])
    divisors = []
    for slot in range(K):
        partner_count = lax.dynamic_slice_in_dim(padded_counts, offsets[slot], C, 0)
        divisors.append(jnp.maximum(jnp.minimum(seg_counts, partner_count), 1).astype(jnp.float32))
    divisor = jnp.stack(divisors, axis=1)
    cross = stacked / divisor[:, :, None]
    delay = delay_table(0, F, L, LAGS, F)
    return jnp.einsum('ckf,fl->ckl', cross, delay, precision=lax.Precision.HIGHEST)
```

```python
import functools
import math

import jax
import jax.numpy as jnp
import ml_dtypes
import numpy as np
from jax import lax
from jax.experimental import pallas as pl
from jax.experimental.pallas import tpu as pltpu
from jax.sharding import PartitionSpec as P

HALF = 32
LAGS = 512
F = 2048
W = 128
EPS = 1e-06
MESH = pl.DeviceIdType.MESH
F32 = jnp.float32
BF16 = jnp.bfloat16


def bins_of(freq, first, number):
    u = np.arange(first, first + number)
    return u if freq == 0 else F - 1 - u


def fourier_blocks(length, chunks):
    t = np.arange(length // 2)[:, None]
    out = np.empty((2, chunks + 1, length // 2, 2 * W), ml_dtypes.bfloat16)
    cos = np.cos(2.0 * math.pi * np.arange(length) / length)
    sin = np.sin(2.0 * math.pi * np.arange(length) / length)
    for freq in range(2):
        for p in range(chunks + 1):
            phase = t * bins_of(freq, p * W, W)[None, :] % length
            out[freq, p, :, :W] = cos[phase].astype(np.float32).astype(ml_dtypes.bfloat16)
            out[freq, p, :, W:] = (-sin[phase]).astype(np.float32).astype(ml_dtypes.bfloat16)
    return out


def delay_blocks(length, chunks):
    shifts = np.arange(LAGS)[None, :] - LAGS // 2
    out = np.empty((2, chunks, 2 * W, LAGS), ml_dtypes.bfloat16)
    for freq in range(2):
        sign = -1.0 if freq == 0 else 1.0
        for q in range(chunks):
            phase = bins_of(freq, q * W, W)[:, None] * shifts % length * (2.0 * math.pi / length)
            out[freq, q, :W] = (np.cos(phase) / math.sqrt(F)).astype(np.float32)
            out[freq, q, W:] = (sign * np.sin(phase) / math.sqrt(F)).astype(np.float32)
    return out


def dot(a, b):
    return jnp.dot(a, b, preferred_element_type=F32)


def iota(shape, dim):
    return lax.broadcasted_iota(jnp.int32, shape, dim)


def kernel(
    nz, ns, segs, chunks, slots, offs, tr, dead, cnt, four, delay, out,
    table, dly, spec, power, own, recv, sel, mask, total, hoth, hrecv, fsend, frecv, vsum, srecv,
    tab_sem, dly_sem, w_send, w_recv, h_send, h_recv, f_send, f_recv, s_send, s_recv,
):
    z = lax.axis_index("chan")
    s_me = lax.axis_index("seg")
    fq = lax.axis_index("freq")
    up = fq == 1
    half_len = table.shape[1]
    rows = own.shape[1]
    per = W // ns
    step = 2 * fq - 1
    dst = z + step
    src = z - step
    has_dst = jnp.logical_and(dst >= 0, dst < nz)
    has_src = jnp.logical_and(src >= 0, src < nz)
    twin = 1 - fq

    def table_copy(p):
        return pltpu.make_async_copy(four.at[fq, p], table.at[p], tab_sem.at[p])

    for p in range(chunks + 1):
        table_copy(p).start()
    delay_copy = pltpu.make_async_copy(delay.at[fq], dly, dly_sem)
    delay_copy.start()

    barrier = pltpu.get_barrier_semaphore()

    @pl.when(has_dst)
    def _():
        pl.semaphore_signal(barrier, inc=1, device_id={"chan": dst}, device_id_type=MESH)

    @pl.when(has_src)
    def _():
        pl.semaphore_signal(barrier, inc=1, device_id={"chan": src}, device_id_type=MESH)

    pl.semaphore_signal(barrier, inc=1, device_id={"freq": twin}, device_id_type=MESH)
    for d in range(1, ns):
        pl.semaphore_signal(
            barrier, inc=1, device_id={"seg": lax.rem(s_me + d, ns)}, device_id_type=MESH
        )

    peers = ns + has_dst.astype(jnp.int32) + has_src.astype(jnp.int32)
    pl.semaphore_wait(barrier, peers)

    diag = iota((W, W), 0) == iota((W, W), 1)
    cnt_col = jnp.sum(jnp.where(diag, cnt[...], 0).astype(F32), axis=1, keepdims=True)
    live_col = jnp.sum(jnp.where(diag, dead[...], 0).astype(F32), axis=1, keepdims=True)
    for s in range(segs):
        seg_number = (s_me * segs + s).astype(F32)
        valid = jnp.where(seg_number < cnt_col, live_col, 0.0)
        mask[s * W : (s + 1) * W, :] = jnp.broadcast_to(valid, (W, W))
    for k in range(slots):
        target = (iota((W, 2 * W), 0) - step * offs[k] + 2 * W) & (2 * W - 1)
        sel[k * W : (k + 1) * W, :] = jnp.where(iota((W, 2 * W), 1) == target, 1.0, 0.0).astype(BF16)

    @pl.when(jnp.logical_not(has_src))
    def _():
        def clear(q, carry):
            recv[q] = jnp.zeros((rows, 2 * W), BF16)
            return carry

        lax.fori_loop(0, chunks, clear, 0)

    parity = (iota((1, 2 * W), 1) & 1).astype(F32)
    parity = (1.0 - 2.0 * parity) * (1 - 2 * fq).astype(F32)

    def block(p):
        table_copy(p).wait()
        first = dot(tr[:, :half_len], table[p])
        second = dot(tr[:, half_len:], table[p])
        both = first + parity * second
        spec[p] = both
        square = both * both
        power[p + 1] = (square[:, :W] + square[:, W:]).astype(BF16)

    def white_copy(q):
        return pltpu.make_async_remote_copy(
            src_ref=own.at[q], dst_ref=recv.at[q], send_sem=w_send.at[q], recv_sem=w_recv.at[q],
            device_id={"chan": dst}, device_id_type=MESH,
        )

    power[0] = jnp.zeros((rows, W), BF16)
    block(0)
    gap = iota((W, W), 0) - iota((W, W), 1)
    bands = [
        jnp.where(jnp.abs(gap + shift) <= HALF, 1.0, 0.0).astype(BF16) for shift in (-W, 0, W)
    ]

    def whiten(p, carry):
        block(p)
        q = p - 1
        window = dot(power[q], bands[0]) + dot(power[p], bands[1]) + dot(power[p + 1], bands[2])
        number = (jnp.minimum(q * W + iota((1, W), 1), HALF) + HALF + 1).astype(F32)
        factor = mask[...] * lax.rsqrt(window / number + EPS)
        own[q, :, :W] = (spec[q, :, :W] * factor).astype(BF16)
        own[q, :, W:] = (spec[q, :, W:] * factor).astype(BF16)

        @pl.when(has_dst)
        def _():
            white_copy(q).start()

        return carry

    lax.fori_loop(1, chunks + 1, whiten, 0)
    delay_copy.wait()
    total[...] = jnp.zeros_like(total)

    def correlate(q, carry):
        @pl.when(has_src)
        def _():
            white_copy(q).wait_recv()

        re = [None] * slots
        im = [None] * slots
        for s in range(segs):
            at = slice(s * W, (s + 1) * W)
            mine = own[q, at, :]
            pair = dot(sel[...], jnp.concatenate([mine, recv[q, at, :]], axis=0))
            my_re = mine[:, :W].astype(F32)
            my_im = mine[:, W:].astype(F32)
            for k in range(slots):
                pair_re = pair[k * W : (k + 1) * W, :W]
                pair_im = pair[k * W : (k + 1) * W, W:]
                one = my_re * pair_re + my_im * pair_im
                two = my_im * pair_re - my_re * pair_im
                re[k] = one if s == 0 else re[k] + one
                im[k] = two if s == 0 else im[k] + two
        for k in range(slots):
            cross = jnp.concatenate([re[k], im[k]], axis=1).astype(BF16)
            total[k] += dot(cross, dly[q])
        return carry

    lax.fori_loop(0, chunks, correlate, 0)

    gap = iota((W, W), 1) - iota((W, W), 0)
    sends_h = jnp.logical_and(up, z > 0)
    takes_h = jnp.logical_and(up, z < nz - 1)

    def h_copy(k):
        return pltpu.make_async_remote_copy(
            src_ref=hoth.at[k], dst_ref=hrecv.at[k], send_sem=h_send.at[k], recv_sem=h_recv.at[k],
            device_id={"chan": z - 1}, device_id_type=MESH,
        )

    def f_copy(k):
        return pltpu.make_async_remote_copy(
            src_ref=fsend.at[k], dst_ref=frecv.at[k], send_sem=f_send.at[k], recv_sem=f_recv.at[k],
            device_id={"freq": twin}, device_id_type=MESH,
        )

    def s_copy(k, d):
        peer = lax.rem(s_me + d, ns)
        return pltpu.make_async_remote_copy(
            src_ref=vsum.at[k, pl.ds(pl.multiple_of(peer * per, per), per)],
            dst_ref=srecv.at[d - 1, k], send_sem=s_send.at[d - 1, k], recv_sem=s_recv.at[d - 1, k],
            device_id={"seg": peer}, device_id_type=MESH,
        )

    @pl.when(up)
    def _():
        for k in range(slots):
            terms = total[k].astype(BF16)
            hoth[k] = dot(jnp.where(gap == offs[k] - W, 1.0, 0.0).astype(BF16), terms).astype(BF16)

            @pl.when(sends_h)
            def _():
                h_copy(k).start()

            total[k] = dot(jnp.where(gap == offs[k], 1.0, 0.0).astype(BF16), terms)

    half = LAGS // 2
    kept = pl.ds(pl.multiple_of(fq * half, half), half)
    given = pl.ds(pl.multiple_of(twin * half, half), half)
    for k in range(slots):
        @pl.when(takes_h)
        def _():
            h_copy(k).wait_recv()
            total[k] += hrecv[k].astype(F32)

        fsend[k] = total[k, :, given].astype(BF16)
        f_copy(k).start()
    for k in range(slots):
        f_copy(k).wait_recv()
        merged = total[k, :, kept] + frecv[k].astype(F32)
        total[k, :, kept] = merged
        vsum[k] = merged.astype(BF16)
        for d in range(1, ns):
            s_copy(k, d).start()
    for k in range(slots):
        result = total[k, pl.ds(pl.multiple_of(s_me * per, per), per), kept]
        for d in range(1, ns):
            s_copy(k, d).wait_recv()
            result += srecv[d - 1, k].astype(F32)
        out[k] = result

    @pl.when(has_dst)
    def _():
        def drain(q, carry):
            white_copy(q).wait_send()
            return carry

        lax.fori_loop(0, chunks, drain, 0)

    for k in range(slots):
        @pl.when(sends_h)
        def _():
            h_copy(k).wait_send()

        f_copy(k).wait_send()
        for d in range(1, ns):
            s_copy(k, d).wait_send()


def shards(traces, dead_mask, seg_counts, offsets):
    segs, chans, length = traces.shape
    nz, ns = lax.axis_size("chan"), lax.axis_size("seg")
    slots = offsets.shape[0]
    chunks = F // 2 // W
    rows = segs * chans
    per = chans // ns
    half = LAGS // 2
    vmem = pl.BlockSpec(memory_space=pltpu.VMEM)
    hbm = pl.BlockSpec(memory_space=pl.ANY)
    dma = pltpu.SemaphoreType.DMA
    terms = pl.pallas_call(
        functools.partial(kernel, nz, ns, segs, chunks, slots),
        out_shape=jax.ShapeDtypeStruct((slots, per, half), F32),
        in_specs=[pl.BlockSpec(memory_space=pltpu.SMEM), vmem, vmem, vmem, hbm, hbm],
        out_specs=vmem,
        scratch_shapes=[
            pltpu.VMEM((chunks + 1, length // 2, 2 * W), BF16),
            pltpu.VMEM((chunks, 2 * W, LAGS), BF16),
            pltpu.VMEM((chunks + 1, rows, 2 * W), F32),
            pltpu.VMEM((chunks + 2, rows, W), BF16),
            pltpu.VMEM((chunks, rows, 2 * W), BF16),
            pltpu.VMEM((chunks, rows, 2 * W), BF16),
            pltpu.VMEM((slots * W, 2 * W), BF16),
            pltpu.VMEM((rows, W), F32),
            pltpu.VMEM((slots, W, LAGS), F32),
            pltpu.VMEM((slots, W, LAGS), BF16),
            pltpu.VMEM((slots, W, LAGS), BF16),
            pltpu.VMEM((slots, W, half), BF16),
            pltpu.VMEM((slots, W, half), BF16),
            pltpu.VMEM((slots, W, half), BF16),
            pltpu.VMEM((max(ns - 1, 1), slots, per, half), BF16),
            dma((chunks + 1,)),
            dma,
            dma((chunks,)),
            dma((chunks,)),
            dma((slots,)),
            dma((slots,)),
            dma((slots,)),
            dma((slots,)),
            dma((max(ns - 1, 1), slots)),
            dma((max(ns - 1, 1), slots)),
        ],
        compiler_params=pltpu.CompilerParams(
            collective_id=0, has_side_effects=True, vmem_limit_bytes=56 * 1024 * 1024
        ),
    )(
        offsets,
        traces.reshape(rows, length),
        dead_mask.reshape(1, chans),
        seg_counts.reshape(1, chans),
        jnp.asarray(fourier_blocks(length, chunks)),
        jnp.asarray(delay_blocks(length, chunks)),
    )
    counts = seg_counts.astype(F32)
    after = lax.ppermute(counts, "chan", [(i + 1, i) for i in range(nz - 1)])
    both = jnp.concatenate([counts, after])
    first = lax.axis_index("seg") * per
    mine = lax.dynamic_slice_in_dim(counts, first, per)
    others = jnp.stack(
        [lax.dynamic_slice_in_dim(both, first + offsets[k], per) for k in range(slots)], axis=1
    )
    divisor = jnp.maximum(jnp.minimum(mine[:, None], others), 1.0)
    return jnp.transpose(terms, (1, 0, 2)) / divisor[:, :, None]


def solution(mesh):
    in_specs = (
        P("seg", ("groups", "chan"), None),
        P(("groups", "chan")),
        P(("groups", "chan")),
        P(),
    )
    out_specs = P(("groups", "chan", "seg"), None, "freq")
    return jax.shard_map(shards, mesh=mesh, in_specs=in_specs, out_specs=out_specs, check_vma=False)
```

```python
import functools
import math

import jax
import jax.numpy as jnp
import ml_dtypes
import numpy as np
from jax import lax
from jax.experimental import pallas as pl
from jax.experimental.pallas import tpu as pltpu
from jax.sharding import PartitionSpec as P

HALF = 32
LAGS = 512
F = 2048
W = 128
EPS = 1e-06
MESH = pl.DeviceIdType.MESH
F32 = jnp.float32
BF16 = jnp.bfloat16


def bins_of(freq, first, number):
    u = np.arange(first, first + number)
    return u if freq == 0 else F - 1 - u


def fourier_blocks(length, chunks):
    t = np.arange(length // 2)[:, None]
    out = np.empty((2, chunks + 1, length // 2, 2 * W), ml_dtypes.bfloat16)
    cos = np.cos(2.0 * math.pi * np.arange(length) / length)
    sin = np.sin(2.0 * math.pi * np.arange(length) / length)
    for freq in range(2):
        for p in range(chunks + 1):
            phase = t * bins_of(freq, p * W, W)[None, :] % length
            out[freq, p, :, :W] = cos[phase].astype(np.float32).astype(ml_dtypes.bfloat16)
            out[freq, p, :, W:] = (-sin[phase]).astype(np.float32).astype(ml_dtypes.bfloat16)
    return out


def delay_blocks(length, chunks):
    shifts = np.arange(LAGS)[None, :] - LAGS // 2
    out = np.empty((2, chunks, 2 * W, LAGS), ml_dtypes.bfloat16)
    for freq in range(2):
        sign = -1.0 if freq == 0 else 1.0
        for q in range(chunks):
            phase = bins_of(freq, q * W, W)[:, None] * shifts % length * (2.0 * math.pi / length)
            out[freq, q, :W] = (np.cos(phase) / math.sqrt(F)).astype(np.float32)
            out[freq, q, W:] = (sign * np.sin(phase) / math.sqrt(F)).astype(np.float32)
    return out


def dot(a, b):
    return jnp.dot(a, b, preferred_element_type=F32)


def iota(shape, dim):
    return lax.broadcasted_iota(jnp.int32, shape, dim)


def kernel(
    nz, ns, segs, chunks, slots, offs, traces, dead, cnt, four, delay, out,
    tr, crecv, inverse, table, dly, spec, power, own, recv, sel, mask, total, hoth, hrecv, fsend, frecv, vsum, srecv,
    tr_sem, c_send, c_recv, tab_sem, dly_sem, w_send, w_recv, h_send, h_recv, f_send, f_recv, s_send, s_recv,
):
    z = lax.axis_index("chan")
    s_me = lax.axis_index("seg")
    fq = lax.axis_index("freq")
    up = fq == 1
    half_len = table.shape[1]
    rows = own.shape[1]
    per = W // ns
    step = 2 * fq - 1
    dst = z + step
    src = z - step
    has_dst = jnp.logical_and(dst >= 0, dst < nz)
    has_src = jnp.logical_and(src >= 0, src < nz)
    twin = 1 - fq

    def table_copy(p):
        return pltpu.make_async_copy(four.at[fq, p], table.at[p], tab_sem.at[p])

    def trace_copy(s):
        return pltpu.make_async_copy(
            traces.at[pl.ds(s * W, W)], tr.at[pl.ds(s * W, W)], tr_sem.at[s]
        )

    table_copy(0).start()
    for s in range(segs):
        trace_copy(s).start()
    for p in range(1, chunks + 1):
        table_copy(p).start()
    delay_copy = pltpu.make_async_copy(delay.at[fq], dly, dly_sem)
    delay_copy.start()

    barrier = pltpu.get_barrier_semaphore()

    @pl.when(has_dst)
    def _():
        pl.semaphore_signal(barrier, inc=1, device_id={"chan": dst}, device_id_type=MESH)

    @pl.when(has_src)
    def _():
        pl.semaphore_signal(barrier, inc=1, device_id={"chan": src}, device_id_type=MESH)

    pl.semaphore_signal(barrier, inc=1, device_id={"freq": twin}, device_id_type=MESH)
    for d in range(1, ns):
        pl.semaphore_signal(
            barrier, inc=1, device_id={"seg": lax.rem(s_me + d, ns)}, device_id_type=MESH
        )

    diag = iota((W, W), 0) == iota((W, W), 1)
    cnt_col = jnp.sum(jnp.where(diag, cnt[...], 0).astype(F32), axis=1, keepdims=True)
    live_col = jnp.sum(jnp.where(diag, dead[...], 0).astype(F32), axis=1, keepdims=True)
    for s in range(segs):
        seg_number = (s_me * segs + s).astype(F32)
        valid = jnp.where(seg_number < cnt_col, live_col, 0.0)
        mask[s * W : (s + 1) * W, :] = jnp.broadcast_to(valid, (W, W))
    for k in range(slots):
        target = (iota((W, 2 * W), 0) - step * offs[k] + 2 * W) & (2 * W - 1)
        sel[k * W : (k + 1) * W, :] = jnp.where(iota((W, 2 * W), 1) == target, 1.0, 0.0).astype(BF16)

    @pl.when(jnp.logical_not(has_src))
    def _():
        def clear(q, carry):
            recv[q] = jnp.zeros((rows, 2 * W), BF16)
            return carry

        lax.fori_loop(0, chunks, clear, 0)
        crecv[...] = jnp.zeros_like(crecv)

    parity = (iota((1, 2 * W), 1) & 1).astype(F32)
    parity = (1.0 - 2.0 * parity) * (1 - 2 * fq).astype(F32)

    def block(p):
        table_copy(p).wait()
        first = dot(tr[:, :half_len], table[p])
        second = dot(tr[:, half_len:], table[p])
        both = first + parity * second
        spec[p] = both
        square = both * both
        power[p + 1] = (square[:, :W] + square[:, W:]).astype(BF16)

    def white_copy(q):
        return pltpu.make_async_remote_copy(
            src_ref=own.at[q], dst_ref=recv.at[q], send_sem=w_send.at[q], recv_sem=w_recv.at[q],
            device_id={"chan": dst}, device_id_type=MESH,
        )

    count_copy = pltpu.make_async_remote_copy(
        src_ref=cnt, dst_ref=crecv, send_sem=c_send, recv_sem=c_recv,
        device_id={"chan": dst}, device_id_type=MESH,
    )
    power[0] = jnp.zeros((rows, W), BF16)
    for s in range(segs):
        trace_copy(s).wait()
    block(0)
    peers = ns + has_dst.astype(jnp.int32) + has_src.astype(jnp.int32)
    pl.semaphore_wait(barrier, peers)

    @pl.when(has_dst)
    def _():
        count_copy.start()

    gap = iota((W, W), 0) - iota((W, W), 1)
    bands = [
        jnp.where(jnp.abs(gap + shift) <= HALF, 1.0, 0.0).astype(BF16) for shift in (-W, 0, W)
    ]

    def whiten(p, carry):
        block(p)
        q = p - 1
        window = dot(power[q], bands[0]) + dot(power[p], bands[1]) + dot(power[p + 1], bands[2])
        number = (jnp.minimum(q * W + iota((1, W), 1), HALF) + HALF + 1).astype(F32)
        factor = mask[...] * lax.rsqrt(window / number + EPS)
        own[q, :, :W] = (spec[q, :, :W] * factor).astype(BF16)
        own[q, :, W:] = (spec[q, :, W:] * factor).astype(BF16)

        @pl.when(has_dst)
        def _():
            white_copy(q).start()

        return carry

    lax.fori_loop(1, chunks + 1, whiten, 0)
    delay_copy.wait()
    total[...] = jnp.zeros_like(total)

    @pl.when(has_src)
    def _():
        count_copy.wait_recv()

    counts = jnp.concatenate([cnt[...], crecv[...]], axis=1)
    for k in range(slots):
        target = (iota((W, 2 * W), 0) - step * offs[k] + 2 * W) & (2 * W - 1)
        partner = jnp.where(iota((W, 2 * W), 1) == target, counts, 0).astype(F32)
        fewer = jnp.minimum(cnt_col, jnp.sum(partner, axis=1, keepdims=True))
        inverse[k] = jnp.broadcast_to(1.0 / jnp.maximum(fewer, 1.0), (W, W))

    def correlate(q, carry):
        @pl.when(has_src)
        def _():
            white_copy(q).wait_recv()

        re = [None] * slots
        im = [None] * slots
        for s in range(segs):
            at = slice(s * W, (s + 1) * W)
            mine = own[q, at, :]
            pair = dot(sel[...], jnp.concatenate([mine, recv[q, at, :]], axis=0))
            my_re = mine[:, :W].astype(F32)
            my_im = mine[:, W:].astype(F32)
            for k in range(slots):
                pair_re = pair[k * W : (k + 1) * W, :W]
                pair_im = pair[k * W : (k + 1) * W, W:]
                one = my_re * pair_re + my_im * pair_im
                two = my_im * pair_re - my_re * pair_im
                re[k] = one if s == 0 else re[k] + one
                im[k] = two if s == 0 else im[k] + two
        for k in range(slots):
            scale = inverse[k]
            cross = jnp.concatenate([re[k] * scale, im[k] * scale], axis=1).astype(BF16)
            total[k] += dot(cross, dly[q])
        return carry

    lax.fori_loop(0, chunks, correlate, 0)

    gap = iota((W, W), 1) - iota((W, W), 0)
    sends_h = jnp.logical_and(up, z > 0)
    takes_h = jnp.logical_and(up, z < nz - 1)

    def h_copy(k):
        return pltpu.make_async_remote_copy(
            src_ref=hoth.at[k], dst_ref=hrecv.at[k], send_sem=h_send.at[k], recv_sem=h_recv.at[k],
            device_id={"chan": z - 1}, device_id_type=MESH,
        )

    def f_copy(k):
        return pltpu.make_async_remote_copy(
            src_ref=fsend.at[k], dst_ref=frecv.at[k], send_sem=f_send.at[k], recv_sem=f_recv.at[k],
            device_id={"freq": twin}, device_id_type=MESH,
        )

    def s_copy(k, d):
        peer = lax.rem(s_me + d, ns)
        return pltpu.make_async_remote_copy(
            src_ref=vsum.at[k, pl.ds(pl.multiple_of(peer * per, per), per)],
            dst_ref=srecv.at[d - 1, k], send_sem=s_send.at[d - 1, k], recv_sem=s_recv.at[d - 1, k],
            device_id={"seg": peer}, device_id_type=MESH,
        )

    @pl.when(up)
    def _():
        for k in range(slots):
            terms = total[k].astype(BF16)
            hoth[k] = dot(jnp.where(gap == offs[k] - W, 1.0, 0.0).astype(BF16), terms).astype(BF16)

            @pl.when(sends_h)
            def _():
                h_copy(k).start()

            total[k] = dot(jnp.where(gap == offs[k], 1.0, 0.0).astype(BF16), terms)

    half = LAGS // 2
    kept = pl.ds(pl.multiple_of(fq * half, half), half)
    given = pl.ds(pl.multiple_of(twin * half, half), half)
    for k in range(slots):
        @pl.when(takes_h)
        def _():
            h_copy(k).wait_recv()
            total[k] += hrecv[k].astype(F32)

        fsend[k] = total[k, :, given].astype(BF16)
        f_copy(k).start()
    for k in range(slots):
        f_copy(k).wait_recv()
        merged = total[k, :, kept] + frecv[k].astype(F32)
        total[k, :, kept] = merged
        vsum[k] = merged.astype(BF16)
        for d in range(1, ns):
            s_copy(k, d).start()
    for k in range(slots):
        result = total[k, pl.ds(pl.multiple_of(s_me * per, per), per), kept]
        for d in range(1, ns):
            s_copy(k, d).wait_recv()
            result += srecv[d - 1, k].astype(F32)
        out[:, k, :] = result

    @pl.when(has_dst)
    def _():
        def drain(q, carry):
            white_copy(q).wait_send()
            return carry

        lax.fori_loop(0, chunks, drain, 0)
        count_copy.wait_send()

    for k in range(slots):
        @pl.when(sends_h)
        def _():
            h_copy(k).wait_send()

        f_copy(k).wait_send()
        for d in range(1, ns):
            s_copy(k, d).wait_send()


def shards(traces, dead_mask, seg_counts, offsets):
    segs, chans, length = traces.shape
    nz, ns = lax.axis_size("chan"), lax.axis_size("seg")
    slots = offsets.shape[0]
    chunks = F // 2 // W
    rows = segs * chans
    per = chans // ns
    half = LAGS // 2
    vmem = pl.BlockSpec(memory_space=pltpu.VMEM)
    hbm = pl.BlockSpec(memory_space=pl.ANY)
    dma = pltpu.SemaphoreType.DMA
    return pl.pallas_call(
        functools.partial(kernel, nz, ns, segs, chunks, slots),
        out_shape=jax.ShapeDtypeStruct((per, slots, half), F32),
        in_specs=[pl.BlockSpec(memory_space=pltpu.SMEM), hbm, vmem, vmem, hbm, hbm],
        out_specs=vmem,
        scratch_shapes=[
            pltpu.VMEM((rows, length), BF16),
            pltpu.VMEM((1, chans), jnp.int32),
            pltpu.VMEM((slots, W, W), F32),
            pltpu.VMEM((chunks + 1, length // 2, 2 * W), BF16),
            pltpu.VMEM((chunks, 2 * W, LAGS), BF16),
            pltpu.VMEM((chunks + 1, rows, 2 * W), F32),
            pltpu.VMEM((chunks + 2, rows, W), BF16),
            pltpu.VMEM((chunks, rows, 2 * W), BF16),
            pltpu.VMEM((chunks, rows, 2 * W), BF16),
            pltpu.VMEM((slots * W, 2 * W), BF16),
            pltpu.VMEM((rows, W), F32),
            pltpu.VMEM((slots, W, LAGS), F32),
            pltpu.VMEM((slots, W, LAGS), BF16),
            pltpu.VMEM((slots, W, LAGS), BF16),
            pltpu.VMEM((slots, W, half), BF16),
            pltpu.VMEM((slots, W, half), BF16),
            pltpu.VMEM((slots, W, half), BF16),
            pltpu.VMEM((max(ns - 1, 1), slots, per, half), BF16),
            dma((segs,)),
            dma,
            dma,
            dma((chunks + 1,)),
            dma,
            dma((chunks,)),
            dma((chunks,)),
            dma((slots,)),
            dma((slots,)),
            dma((slots,)),
            dma((slots,)),
            dma((max(ns - 1, 1), slots)),
            dma((max(ns - 1, 1), slots)),
        ],
        compiler_params=pltpu.CompilerParams(
            collective_id=0, has_side_effects=True, vmem_limit_bytes=56 * 1024 * 1024
        ),
    )(
        offsets,
        traces.reshape(rows, length),
        dead_mask.reshape(1, chans),
        seg_counts.reshape(1, chans),
        jnp.asarray(fourier_blocks(length, chunks)),
        jnp.asarray(delay_blocks(length, chunks)),
    )


def solution(mesh):
    in_specs = (
        P("seg", ("groups", "chan"), None),
        P(("groups", "chan")),
        P(("groups", "chan")),
        P(),
    )
    out_specs = P(("groups", "chan", "seg"), None, "freq")
    return jax.shard_map(shards, mesh=mesh, in_specs=in_specs, out_specs=out_specs, check_vma=False)
```

```python
import functools
import math

import jax
import jax.numpy as jnp
import ml_dtypes
import numpy as np
from jax import lax
from jax.experimental import pallas as pl
from jax.experimental.pallas import tpu as pltpu
from jax.sharding import PartitionSpec as P

HALF = 32
LAGS = 512
F = 2048
W = 128
EPS = 1e-06
MESH = pl.DeviceIdType.MESH
F32 = jnp.float32
BF16 = jnp.bfloat16


def bins_of(freq, first, number):
    u = np.arange(first, first + number)
    return u if freq == 0 else F - 1 - u


def fourier_blocks(length, chunks):
    t = np.arange(length // 2)[:, None]
    out = np.empty((2, chunks + 1, length // 2, 2 * W), ml_dtypes.bfloat16)
    cos = np.cos(2.0 * math.pi * np.arange(length) / length)
    sin = np.sin(2.0 * math.pi * np.arange(length) / length)
    for freq in range(2):
        for p in range(chunks + 1):
            phase = t * bins_of(freq, p * W, W)[None, :] % length
            out[freq, p, :, :W] = cos[phase].astype(np.float32).astype(ml_dtypes.bfloat16)
            out[freq, p, :, W:] = (-sin[phase]).astype(np.float32).astype(ml_dtypes.bfloat16)
    return out


def delay_blocks(length, chunks):
    shifts = np.arange(LAGS)[None, :] - LAGS // 2
    out = np.empty((2, chunks, 2 * W, LAGS), ml_dtypes.bfloat16)
    for freq in range(2):
        sign = -1.0 if freq == 0 else 1.0
        for q in range(chunks):
            phase = bins_of(freq, q * W, W)[:, None] * shifts % length * (2.0 * math.pi / length)
            out[freq, q, :W] = (np.cos(phase) / math.sqrt(F)).astype(np.float32)
            out[freq, q, W:] = (sign * np.sin(phase) / math.sqrt(F)).astype(np.float32)
    return out


def dot(a, b):
    return jnp.dot(a, b, preferred_element_type=F32)


def iota(shape, dim):
    return lax.broadcasted_iota(jnp.int32, shape, dim)


def kernel(
    nz, ns, segs, chunks, slots, offs, traces, dead, cnt, four, delay, out,
    tr, crecv, inverse, table, dly, spec, power, own, recv, sel, mask, total, hoth, hrecv, fsend, frecv, vsum, srecv,
    tr_sem, c_send, c_recv, tab_sem, dly_sem, w_send, w_recv, h_send, h_recv, f_send, f_recv, s_send, s_recv,
):
    z = lax.axis_index("chan")
    s_me = lax.axis_index("seg")
    fq = lax.axis_index("freq")
    up = fq == 1
    half_len = table.shape[1]
    rows = own.shape[1]
    per = W // ns
    step = 2 * fq - 1
    dst = z + step
    src = z - step
    has_dst = jnp.logical_and(dst >= 0, dst < nz)
    has_src = jnp.logical_and(src >= 0, src < nz)
    twin = 1 - fq

    def table_copy(p):
        return pltpu.make_async_copy(four.at[fq, p], table.at[p], tab_sem.at[p])

    def trace_copy(s):
        return pltpu.make_async_copy(
            traces.at[pl.ds(s * W, W)], tr.at[pl.ds(s * W, W)], tr_sem.at[s]
        )

    table_copy(0).start()
    for s in range(segs):
        trace_copy(s).start()
    for p in range(1, chunks + 1):
        table_copy(p).start()
    delay_copy = pltpu.make_async_copy(delay.at[fq], dly, dly_sem)
    delay_copy.start()

    sends_h = jnp.logical_and(up, z > 0)
    takes_h = z < nz - 1
    barrier = pltpu.get_barrier_semaphore()

    @pl.when(has_src)
    def _():
        pl.semaphore_signal(barrier, inc=1, device_id={"chan": src}, device_id_type=MESH)

    pl.semaphore_signal(barrier, inc=1, device_id={"freq": twin}, device_id_type=MESH)
    for d in range(1, ns):
        pl.semaphore_signal(
            barrier, inc=1, device_id={"seg": lax.rem(s_me + d, ns)}, device_id_type=MESH
        )

    @pl.when(takes_h)
    def _():
        for d in range(ns):
            giver = {"chan": z + 1, "seg": lax.rem(s_me + d, ns), "freq": 1}
            pl.semaphore_signal(barrier, inc=1, device_id=giver, device_id_type=MESH)

    diag = iota((W, W), 0) == iota((W, W), 1)
    cnt_col = jnp.sum(jnp.where(diag, cnt[...], 0).astype(F32), axis=1, keepdims=True)
    live_col = jnp.sum(jnp.where(diag, dead[...], 0).astype(F32), axis=1, keepdims=True)
    for s in range(segs):
        seg_number = (s_me * segs + s).astype(F32)
        valid = jnp.where(seg_number < cnt_col, live_col, 0.0)
        mask[s * W : (s + 1) * W, :] = jnp.broadcast_to(valid, (W, W))
    for k in range(slots):
        target = (iota((W, 2 * W), 0) - step * offs[k] + 2 * W) & (2 * W - 1)
        sel[k * W : (k + 1) * W, :] = jnp.where(iota((W, 2 * W), 1) == target, 1.0, 0.0).astype(BF16)

    @pl.when(jnp.logical_not(has_src))
    def _():
        def clear(q, carry):
            recv[q] = jnp.zeros((rows, 2 * W), BF16)
            return carry

        lax.fori_loop(0, chunks, clear, 0)
        crecv[...] = jnp.zeros_like(crecv)

    @pl.when(jnp.logical_not(takes_h))
    def _():
        hrecv[...] = jnp.zeros_like(hrecv)

    parity = (iota((1, 2 * W), 1) & 1).astype(F32)
    parity = (1.0 - 2.0 * parity) * (1 - 2 * fq).astype(F32)

    def block(p):
        table_copy(p).wait()
        first = dot(tr[:, :half_len], table[p])
        second = dot(tr[:, half_len:], table[p])
        both = first + parity * second
        spec[p] = both
        square = both * both
        power[p + 1] = (square[:, :W] + square[:, W:]).astype(BF16)

    def white_copy(q):
        return pltpu.make_async_remote_copy(
            src_ref=own.at[q], dst_ref=recv.at[q], send_sem=w_send.at[q], recv_sem=w_recv.at[q],
            device_id={"chan": dst}, device_id_type=MESH,
        )

    count_copy = pltpu.make_async_remote_copy(
        src_ref=cnt, dst_ref=crecv, send_sem=c_send, recv_sem=c_recv,
        device_id={"chan": dst}, device_id_type=MESH,
    )
    power[0] = jnp.zeros((rows, W), BF16)
    for s in range(segs):
        trace_copy(s).wait()
    block(0)
    peers = ns + has_dst.astype(jnp.int32) + 2 * ns * sends_h.astype(jnp.int32)
    pl.semaphore_wait(barrier, peers)

    @pl.when(has_dst)
    def _():
        count_copy.start()

    gap = iota((W, W), 0) - iota((W, W), 1)
    bands = [
        jnp.where(jnp.abs(gap + shift) <= HALF, 1.0, 0.0).astype(BF16) for shift in (-W, 0, W)
    ]

    def whiten(p, carry):
        block(p)
        q = p - 1
        window = dot(power[q], bands[0]) + dot(power[p], bands[1]) + dot(power[p + 1], bands[2])
        number = (jnp.minimum(q * W + iota((1, W), 1), HALF) + HALF + 1).astype(F32)
        factor = mask[...] * lax.rsqrt(window / number + EPS)
        own[q, :, :W] = (spec[q, :, :W] * factor).astype(BF16)
        own[q, :, W:] = (spec[q, :, W:] * factor).astype(BF16)

        @pl.when(has_dst)
        def _():
            white_copy(q).start()

        return carry

    lax.fori_loop(1, chunks + 1, whiten, 0)
    delay_copy.wait()
    total[...] = jnp.zeros_like(total)

    @pl.when(has_src)
    def _():
        count_copy.wait_recv()

    counts = jnp.concatenate([cnt[...], crecv[...]], axis=1)
    for k in range(slots):
        target = (iota((W, 2 * W), 0) - step * offs[k] + 2 * W) & (2 * W - 1)
        partner = jnp.where(iota((W, 2 * W), 1) == target, counts, 0).astype(F32)
        fewer = jnp.minimum(cnt_col, jnp.sum(partner, axis=1, keepdims=True))
        inverse[k] = jnp.broadcast_to(1.0 / jnp.maximum(fewer, 1.0), (W, W))

    def correlate(q, carry):
        @pl.when(has_src)
        def _():
            white_copy(q).wait_recv()

        re = [None] * slots
        im = [None] * slots
        for s in range(segs):
            at = slice(s * W, (s + 1) * W)
            mine = own[q, at, :]
            pair = dot(sel[...], jnp.concatenate([mine, recv[q, at, :]], axis=0))
            my_re = mine[:, :W].astype(F32)
            my_im = mine[:, W:].astype(F32)
            for k in range(slots):
                pair_re = pair[k * W : (k + 1) * W, :W]
                pair_im = pair[k * W : (k + 1) * W, W:]
                one = my_re * pair_re + my_im * pair_im
                two = my_im * pair_re - my_re * pair_im
                re[k] = one if s == 0 else re[k] + one
                im[k] = two if s == 0 else im[k] + two
        for k in range(slots):
            scale = inverse[k]
            cross = jnp.concatenate([re[k] * scale, im[k] * scale], axis=1).astype(BF16)
            total[k] += dot(cross, dly[q])
        return carry

    lax.fori_loop(0, chunks, correlate, 0)

    gap = iota((W, W), 1) - iota((W, W), 0)
    half = LAGS // 2

    def h_copy(d, q):
        peer = lax.rem(s_me + d, ns)
        return pltpu.make_async_remote_copy(
            src_ref=hoth.at[:, pl.ds(pl.multiple_of(peer * per, per), per), q * half : (q + 1) * half],
            dst_ref=hrecv.at[d], send_sem=h_send.at[d, q], recv_sem=h_recv.at[d],
            device_id={"chan": z - 1, "seg": peer, "freq": q}, device_id_type=MESH,
        )

    f_copy = pltpu.make_async_remote_copy(
        src_ref=fsend, dst_ref=frecv, send_sem=f_send, recv_sem=f_recv,
        device_id={"freq": twin}, device_id_type=MESH,
    )

    def s_copy(d):
        peer = lax.rem(s_me + d, ns)
        return pltpu.make_async_remote_copy(
            src_ref=vsum.at[:, pl.ds(pl.multiple_of(peer * per, per), per)],
            dst_ref=srecv.at[d - 1], send_sem=s_send.at[d - 1], recv_sem=s_recv.at[d - 1],
            device_id={"seg": peer}, device_id_type=MESH,
        )

    @pl.when(up)
    def _():
        for k in range(slots):
            moved = dot(jnp.where(gap == offs[k] - W, 1.0, 0.0).astype(BF16), total[k].astype(BF16))
            hoth[k] = moved.astype(BF16)

        @pl.when(sends_h)
        def _():
            for d in reversed(range(ns)):
                for q in range(2):
                    h_copy(d, q).start()

        for k in range(slots):
            total[k] = dot(jnp.where(gap == offs[k], 1.0, 0.0).astype(BF16), total[k].astype(BF16))

    kept = pl.ds(pl.multiple_of(fq * half, half), half)
    given = pl.ds(pl.multiple_of(twin * half, half), half)
    for k in range(slots):
        fsend[k] = total[k, :, given].astype(BF16)
    f_copy.start()
    f_copy.wait_recv()
    for k in range(slots):
        merged = total[k, :, kept] + frecv[k].astype(F32)
        total[k, :, kept] = merged
        vsum[k] = merged.astype(BF16)
    for d in range(1, ns):
        s_copy(d).start()
    for d in range(1, ns):
        s_copy(d).wait_recv()

    @pl.when(takes_h)
    def _():
        for d in range(ns):
            h_copy(d, 0).wait_recv()

    for k in range(slots):
        result = total[k, pl.ds(pl.multiple_of(s_me * per, per), per), kept]
        for d in range(1, ns):
            result += srecv[d - 1, k].astype(F32)
        for d in range(ns):
            result += hrecv[d, k].astype(F32)
        out[k] = result

    @pl.when(has_dst)
    def _():
        def drain(q, carry):
            white_copy(q).wait_send()
            return carry

        lax.fori_loop(0, chunks, drain, 0)
        count_copy.wait_send()

    @pl.when(sends_h)
    def _():
        for d in range(ns):
            for q in range(2):
                h_copy(d, q).wait_send()

    f_copy.wait_send()
    for d in range(1, ns):
        s_copy(d).wait_send()


def shards(traces, dead_mask, seg_counts, offsets):
    segs, chans, length = traces.shape
    nz, ns = lax.axis_size("chan"), lax.axis_size("seg")
    slots = offsets.shape[0]
    chunks = F // 2 // W
    rows = segs * chans
    per = chans // ns
    half = LAGS // 2
    vmem = pl.BlockSpec(memory_space=pltpu.VMEM)
    hbm = pl.BlockSpec(memory_space=pl.ANY)
    dma = pltpu.SemaphoreType.DMA
    terms = pl.pallas_call(
        functools.partial(kernel, nz, ns, segs, chunks, slots),
        out_shape=jax.ShapeDtypeStruct((slots, per, half), F32),
        in_specs=[pl.BlockSpec(memory_space=pltpu.SMEM), hbm, vmem, vmem, hbm, hbm],
        out_specs=vmem,
        scratch_shapes=[
            pltpu.VMEM((rows, length), BF16),
            pltpu.VMEM((1, chans), jnp.int32),
            pltpu.VMEM((slots, W, W), F32),
            pltpu.VMEM((chunks + 1, length // 2, 2 * W), BF16),
            pltpu.VMEM((chunks, 2 * W, LAGS), BF16),
            pltpu.VMEM((chunks + 1, rows, 2 * W), F32),
            pltpu.VMEM((chunks + 2, rows, W), BF16),
            pltpu.VMEM((chunks, rows, 2 * W), BF16),
            pltpu.VMEM((chunks, rows, 2 * W), BF16),
            pltpu.VMEM((slots * W, 2 * W), BF16),
            pltpu.VMEM((rows, W), F32),
            pltpu.VMEM((slots, W, LAGS), F32),
            pltpu.VMEM((slots, W, LAGS), BF16),
            pltpu.VMEM((ns, slots, per, half), BF16),
            pltpu.VMEM((slots, W, half), BF16),
            pltpu.VMEM((slots, W, half), BF16),
            pltpu.VMEM((slots, W, half), BF16),
            pltpu.VMEM((max(ns - 1, 1), slots, per, half), BF16),
            dma((segs,)),
            dma,
            dma,
            dma((chunks + 1,)),
            dma,
            dma((chunks,)),
            dma((chunks,)),
            dma((ns, 2)),
            dma((ns,)),
            dma,
            dma,
            dma((max(ns - 1, 1),)),
            dma((max(ns - 1, 1),)),
        ],
        compiler_params=pltpu.CompilerParams(
            collective_id=0, has_side_effects=True, vmem_limit_bytes=56 * 1024 * 1024
        ),
    )(
        offsets,
        traces.reshape(rows, length),
        dead_mask.reshape(1, chans),
        seg_counts.reshape(1, chans),
        jnp.asarray(fourier_blocks(length, chunks)),
        jnp.asarray(delay_blocks(length, chunks)),
    )
    return jnp.transpose(terms, (1, 0, 2))


def solution(mesh):
    in_specs = (
        P("seg", ("groups", "chan"), None),
        P(("groups", "chan")),
        P(("groups", "chan")),
        P(),
    )
    out_specs = P(("groups", "chan", "seg"), None, "freq")
    return jax.shard_map(shards, mesh=mesh, in_specs=in_specs, out_specs=out_specs, check_vma=False)
```

```python
import functools
import math

import jax
import jax.numpy as jnp
import ml_dtypes
import numpy as np
from jax import lax
from jax.experimental import pallas as pl
from jax.experimental.pallas import tpu as pltpu
from jax.sharding import PartitionSpec as P

HALF = 32
LAGS = 512
F = 2048
W = 128
EPS = 1e-06
MESH = pl.DeviceIdType.MESH
F32 = jnp.float32
BF16 = jnp.bfloat16


def bins_of(freq, first, number):
    u = np.arange(first, first + number)
    return u if freq == 0 else F - 1 - u


def fourier_blocks(length, chunks):
    t = np.arange(length // 2)[:, None]
    out = np.empty((2, chunks + 1, length // 2, 2 * W), ml_dtypes.bfloat16)
    cos = np.cos(2.0 * math.pi * np.arange(length) / length)
    sin = np.sin(2.0 * math.pi * np.arange(length) / length)
    for freq in range(2):
        for p in range(chunks + 1):
            phase = t * bins_of(freq, p * W, W)[None, :] % length
            out[freq, p, :, :W] = cos[phase].astype(np.float32).astype(ml_dtypes.bfloat16)
            out[freq, p, :, W:] = (-sin[phase]).astype(np.float32).astype(ml_dtypes.bfloat16)
    return out


def delay_blocks(length, chunks):
    shifts = np.arange(LAGS)[None, :] - LAGS // 2
    out = np.empty((2, chunks, 2 * W, LAGS), ml_dtypes.bfloat16)
    for freq in range(2):
        sign = -1.0 if freq == 0 else 1.0
        for q in range(chunks):
            phase = bins_of(freq, q * W, W)[:, None] * shifts % length * (2.0 * math.pi / length)
            out[freq, q, :W] = (np.cos(phase) / math.sqrt(F)).astype(np.float32)
            out[freq, q, W:] = (sign * np.sin(phase) / math.sqrt(F)).astype(np.float32)
    return out


def dot(a, b):
    return jnp.dot(a, b, preferred_element_type=F32)


def iota(shape, dim):
    return lax.broadcasted_iota(jnp.int32, shape, dim)


def kernel(
    nz, ns, segs, chunks, slots, offs, traces, dead, cnt, four, delay, out,
    tr, crecv, inverse, table, dly, spec, power, own, recv, sel, mask, total, hoth, hrecv, fsend, frecv, vsum, srecv,
    tr_sem, c_send, c_recv, tab_sem, dly_sem, w_send, w_recv, h_send, h_recv, f_send, f_recv, s_send, s_recv,
):
    z = lax.axis_index("chan")
    s_me = lax.axis_index("seg")
    fq = lax.axis_index("freq")
    up = fq == 1
    half_len = table.shape[1]
    rows = own.shape[1]
    per = W // ns
    step = 2 * fq - 1
    dst = z + step
    src = z - step
    has_dst = jnp.logical_and(dst >= 0, dst < nz)
    has_src = jnp.logical_and(src >= 0, src < nz)
    twin = 1 - fq

    def table_copy(p):
        return pltpu.make_async_copy(four.at[fq, p], table.at[p], tab_sem.at[p])

    def trace_copy(s):
        return pltpu.make_async_copy(
            traces.at[pl.ds(s * W, W)], tr.at[pl.ds(s * W, W)], tr_sem.at[s]
        )

    table_copy(0).start()
    trace_copy(0).start()
    table_copy(1).start()
    for s in range(1, segs):
        trace_copy(s).start()
    for p in range(2, chunks + 1):
        table_copy(p).start()
    delay_copy = pltpu.make_async_copy(delay.at[fq], dly, dly_sem)
    delay_copy.start()

    sends_h = jnp.logical_and(up, z > 0)
    takes_h = z < nz - 1
    barrier = pltpu.get_barrier_semaphore()

    @pl.when(has_src)
    def _():
        pl.semaphore_signal(barrier, inc=1, device_id={"chan": src}, device_id_type=MESH)

    pl.semaphore_signal(barrier, inc=1, device_id={"freq": twin}, device_id_type=MESH)
    for d in range(1, ns):
        pl.semaphore_signal(
            barrier, inc=1, device_id={"seg": lax.rem(s_me + d, ns)}, device_id_type=MESH
        )

    @pl.when(takes_h)
    def _():
        for d in range(ns):
            giver = {"chan": z + 1, "seg": lax.rem(s_me + d, ns), "freq": 1}
            pl.semaphore_signal(barrier, inc=1, device_id=giver, device_id_type=MESH)

    diag = iota((W, W), 0) == iota((W, W), 1)
    cnt_col = jnp.sum(jnp.where(diag, cnt[...], 0).astype(F32), axis=1, keepdims=True)
    live_col = jnp.sum(jnp.where(diag, dead[...], 0).astype(F32), axis=1, keepdims=True)
    for s in range(segs):
        seg_number = (s_me * segs + s).astype(F32)
        valid = jnp.where(seg_number < cnt_col, live_col, 0.0)
        mask[s * W : (s + 1) * W, :] = jnp.broadcast_to(valid, (W, W))
    for k in range(slots):
        target = (iota((W, 2 * W), 0) - step * offs[k] + 2 * W) & (2 * W - 1)
        sel[k * W : (k + 1) * W, :] = jnp.where(iota((W, 2 * W), 1) == target, 1.0, 0.0).astype(BF16)

    @pl.when(jnp.logical_not(has_src))
    def _():
        def clear(q, carry):
            recv[q] = jnp.zeros((rows, 2 * W), BF16)
            return carry

        lax.fori_loop(0, chunks, clear, 0)
        crecv[...] = jnp.zeros_like(crecv)

    @pl.when(jnp.logical_not(takes_h))
    def _():
        hrecv[...] = jnp.zeros_like(hrecv)

    parity = (iota((1, 2 * W), 1) & 1).astype(F32)
    parity = (1.0 - 2.0 * parity) * (1 - 2 * fq).astype(F32)

    gap = iota((W, W), 0) - iota((W, W), 1)
    bands = [
        jnp.where(jnp.abs(gap + shift) <= HALF, 1.0, 0.0).astype(BF16) for shift in (-W, 0, W)
    ]

    def block(p, at):
        first = dot(tr[at, :half_len], table[p])
        second = dot(tr[at, half_len:], table[p])
        both = first + parity * second
        spec[p, at, :] = both
        square = both * both
        power[p + 1, at, :] = (square[:, :W] + square[:, W:]).astype(BF16)

    def whiten(q, at):
        window = (
            dot(power[q, at, :], bands[0]) + dot(power[q + 1, at, :], bands[1])
            + dot(power[q + 2, at, :], bands[2])
        )
        number = (jnp.minimum(q * W + iota((1, W), 1), HALF) + HALF + 1).astype(F32)
        factor = mask[at, :] * lax.rsqrt(window / number + EPS)
        own[q, at, :W] = (spec[q, at, :W] * factor).astype(BF16)
        own[q, at, W:] = (spec[q, at, W:] * factor).astype(BF16)

    def white_copy(q, at):
        return pltpu.make_async_remote_copy(
            src_ref=own.at[q, at], dst_ref=recv.at[q, at],
            send_sem=w_send.at[q], recv_sem=w_recv.at[q],
            device_id={"chan": dst}, device_id_type=MESH,
        )

    def send(q, at):
        @pl.when(has_dst)
        def _():
            white_copy(q, at).start()

    whole = pl.ds(0, rows)

    def rows_of(s):
        return pl.ds(pl.multiple_of(s * W, W), W)

    count_copy = pltpu.make_async_remote_copy(
        src_ref=cnt, dst_ref=crecv, send_sem=c_send, recv_sem=c_recv,
        device_id={"chan": dst}, device_id_type=MESH,
    )
    power[0] = jnp.zeros((rows, W), BF16)
    table_copy(0).wait()
    trace_copy(0).wait()
    block(0, rows_of(0))
    table_copy(1).wait()
    block(1, rows_of(0))
    whiten(0, rows_of(0))
    peers = ns + has_dst.astype(jnp.int32) + 2 * ns * sends_h.astype(jnp.int32)
    pl.semaphore_wait(barrier, peers)

    @pl.when(has_dst)
    def _():
        count_copy.start()

    send(0, rows_of(0))

    def first_chunk(s, carry):
        trace_copy(s).wait()
        block(0, rows_of(s))
        block(1, rows_of(s))
        whiten(0, rows_of(s))
        send(0, rows_of(s))
        return carry

    def second_chunk(s, carry):
        block(2, rows_of(s))
        whiten(1, rows_of(s))
        send(1, rows_of(s))
        return carry

    def later_chunk(p, carry):
        table_copy(p).wait()
        block(p, whole)
        whiten(p - 1, whole)
        send(p - 1, whole)
        return carry

    lax.fori_loop(1, segs, first_chunk, 0)
    table_copy(2).wait()
    lax.fori_loop(0, segs, second_chunk, 0)
    lax.fori_loop(3, chunks + 1, later_chunk, 0)
    delay_copy.wait()
    total[...] = jnp.zeros_like(total)

    @pl.when(has_src)
    def _():
        count_copy.wait_recv()

    counts = jnp.concatenate([cnt[...], crecv[...]], axis=1)
    for k in range(slots):
        target = (iota((W, 2 * W), 0) - step * offs[k] + 2 * W) & (2 * W - 1)
        partner = jnp.where(iota((W, 2 * W), 1) == target, counts, 0).astype(F32)
        fewer = jnp.minimum(cnt_col, jnp.sum(partner, axis=1, keepdims=True))
        inverse[k] = jnp.broadcast_to(1.0 / jnp.maximum(fewer, 1.0), (W, W))

    def correlate(q, carry):
        @pl.when(has_src)
        def _():
            white_copy(q, whole).wait_recv()

        re = [None] * slots
        im = [None] * slots
        for s in range(segs):
            at = slice(s * W, (s + 1) * W)
            mine = own[q, at, :]
            pair = dot(sel[...], jnp.concatenate([mine, recv[q, at, :]], axis=0))
            my_re = mine[:, :W].astype(F32)
            my_im = mine[:, W:].astype(F32)
            for k in range(slots):
                pair_re = pair[k * W : (k + 1) * W, :W]
                pair_im = pair[k * W : (k + 1) * W, W:]
                one = my_re * pair_re + my_im * pair_im
                two = my_im * pair_re - my_re * pair_im
                re[k] = one if s == 0 else re[k] + one
                im[k] = two if s == 0 else im[k] + two
        for k in range(slots):
            scale = inverse[k]
            cross = jnp.concatenate([re[k] * scale, im[k] * scale], axis=1).astype(BF16)
            total[k] += dot(cross, dly[q])
        return carry

    lax.fori_loop(0, chunks, correlate, 0)

    gap = iota((W, W), 1) - iota((W, W), 0)
    half = LAGS // 2

    def h_copy(d, q):
        peer = lax.rem(s_me + d, ns)
        return pltpu.make_async_remote_copy(
            src_ref=hoth.at[:, pl.ds(pl.multiple_of(peer * per, per), per), q * half : (q + 1) * half],
            dst_ref=hrecv.at[d], send_sem=h_send.at[d, q], recv_sem=h_recv.at[d],
            device_id={"chan": z - 1, "seg": peer, "freq": q}, device_id_type=MESH,
        )

    f_copy = pltpu.make_async_remote_copy(
        src_ref=fsend, dst_ref=frecv, send_sem=f_send, recv_sem=f_recv,
        device_id={"freq": twin}, device_id_type=MESH,
    )

    def s_copy(d):
        peer = lax.rem(s_me + d, ns)
        return pltpu.make_async_remote_copy(
            src_ref=vsum.at[:, pl.ds(pl.multiple_of(peer * per, per), per)],
            dst_ref=srecv.at[d - 1], send_sem=s_send.at[d - 1], recv_sem=s_recv.at[d - 1],
            device_id={"seg": peer}, device_id_type=MESH,
        )

    @pl.when(up)
    def _():
        for k in range(slots):
            moved = dot(jnp.where(gap == offs[k] - W, 1.0, 0.0).astype(BF16), total[k].astype(BF16))
            hoth[k] = moved.astype(BF16)

        @pl.when(sends_h)
        def _():
            for d in reversed(range(ns)):
                for q in range(2):
                    h_copy(d, q).start()

        for k in range(slots):
            total[k] = dot(jnp.where(gap == offs[k], 1.0, 0.0).astype(BF16), total[k].astype(BF16))

    kept = pl.ds(pl.multiple_of(fq * half, half), half)
    given = pl.ds(pl.multiple_of(twin * half, half), half)
    for k in range(slots):
        fsend[k] = total[k, :, given].astype(BF16)
    f_copy.start()
    f_copy.wait_recv()
    for k in range(slots):
        merged = total[k, :, kept] + frecv[k].astype(F32)
        total[k, :, kept] = merged
        vsum[k] = merged.astype(BF16)
    for d in range(1, ns):
        s_copy(d).start()
    for d in range(1, ns):
        s_copy(d).wait_recv()

    @pl.when(takes_h)
    def _():
        for d in range(ns):
            h_copy(d, 0).wait_recv()

    for k in range(slots):
        result = total[k, pl.ds(pl.multiple_of(s_me * per, per), per), kept]
        for d in range(1, ns):
            result += srecv[d - 1, k].astype(F32)
        for d in range(ns):
            result += hrecv[d, k].astype(F32)
        out[k] = result

    @pl.when(has_dst)
    def _():
        def drain(q, carry):
            white_copy(q, whole).wait_send()
            return carry

        lax.fori_loop(0, chunks, drain, 0)
        count_copy.wait_send()

    @pl.when(sends_h)
    def _():
        for d in range(ns):
            for q in range(2):
                h_copy(d, q).wait_send()

    f_copy.wait_send()
    for d in range(1, ns):
        s_copy(d).wait_send()


def shards(traces, dead_mask, seg_counts, offsets):
    segs, chans, length = traces.shape
    nz, ns = lax.axis_size("chan"), lax.axis_size("seg")
    slots = offsets.shape[0]
    chunks = F // 2 // W
    rows = segs * chans
    per = chans // ns
    half = LAGS // 2
    vmem = pl.BlockSpec(memory_space=pltpu.VMEM)
    hbm = pl.BlockSpec(memory_space=pl.ANY)
    dma = pltpu.SemaphoreType.DMA
    terms = pl.pallas_call(
        functools.partial(kernel, nz, ns, segs, chunks, slots),
        out_shape=jax.ShapeDtypeStruct((slots, per, half), F32),
        in_specs=[pl.BlockSpec(memory_space=pltpu.SMEM), hbm, vmem, vmem, hbm, hbm],
        out_specs=vmem,
        scratch_shapes=[
            pltpu.VMEM((rows, length), BF16),
            pltpu.VMEM((1, chans), jnp.int32),
            pltpu.VMEM((slots, W, W), F32),
            pltpu.VMEM((chunks + 1, length // 2, 2 * W), BF16),
            pltpu.VMEM((chunks, 2 * W, LAGS), BF16),
            pltpu.VMEM((chunks + 1, rows, 2 * W), F32),
            pltpu.VMEM((chunks + 2, rows, W), BF16),
            pltpu.VMEM((chunks, rows, 2 * W), BF16),
            pltpu.VMEM((chunks, rows, 2 * W), BF16),
            pltpu.VMEM((slots * W, 2 * W), BF16),
            pltpu.VMEM((rows, W), F32),
            pltpu.VMEM((slots, W, LAGS), F32),
            pltpu.VMEM((slots, W, LAGS), BF16),
            pltpu.VMEM((ns, slots, per, half), BF16),
            pltpu.VMEM((slots, W, half), BF16),
            pltpu.VMEM((slots, W, half), BF16),
            pltpu.VMEM((slots, W, half), BF16),
            pltpu.VMEM((max(ns - 1, 1), slots, per, half), BF16),
            dma((segs,)),
            dma,
            dma,
            dma((chunks + 1,)),
            dma,
            dma((chunks,)),
            dma((chunks,)),
            dma((ns, 2)),
            dma((ns,)),
            dma,
            dma,
            dma((max(ns - 1, 1),)),
            dma((max(ns - 1, 1),)),
        ],
        compiler_params=pltpu.CompilerParams(
            collective_id=0, has_side_effects=True, vmem_limit_bytes=56 * 1024 * 1024
        ),
    )(
        offsets,
        traces.reshape(rows, length),
        dead_mask.reshape(1, chans),
        seg_counts.reshape(1, chans),
        jnp.asarray(fourier_blocks(length, chunks)),
        jnp.asarray(delay_blocks(length, chunks)),
    )
    return jnp.transpose(terms, (1, 0, 2))


def solution(mesh):
    in_specs = (
        P("seg", ("groups", "chan"), None),
        P(("groups", "chan")),
        P(("groups", "chan")),
        P(),
    )
    out_specs = P(("groups", "chan", "seg"), None, "freq")
    return jax.shard_map(shards, mesh=mesh, in_specs=in_specs, out_specs=out_specs, check_vma=False)
```

```python
import functools
import math

import jax
import jax.numpy as jnp
import ml_dtypes
import numpy as np
from jax import lax
from jax.experimental import pallas as pl
from jax.experimental.pallas import tpu as pltpu
from jax.sharding import PartitionSpec as P

HALF = 32
LAGS = 512
F = 2048
W = 128
EPS = 1e-06
MESH = pl.DeviceIdType.MESH
F32 = jnp.float32
BF16 = jnp.bfloat16


def bins_of(freq, first, number):
    u = np.arange(first, first + number)
    return u if freq == 0 else F - 1 - u


def fourier_blocks(length, chunks):
    t = np.arange(length // 2)[:, None]
    out = np.empty((2, chunks + 1, length // 2, 2 * W), ml_dtypes.bfloat16)
    cos = np.cos(2.0 * math.pi * np.arange(length) / length)
    sin = np.sin(2.0 * math.pi * np.arange(length) / length)
    for freq in range(2):
        for p in range(chunks + 1):
            phase = t * bins_of(freq, p * W, W)[None, :] % length
            out[freq, p, :, :W] = cos[phase].astype(np.float32).astype(ml_dtypes.bfloat16)
            out[freq, p, :, W:] = (-sin[phase]).astype(np.float32).astype(ml_dtypes.bfloat16)
    return out


def delay_blocks(length, chunks):
    shifts = np.arange(LAGS)[None, :] - LAGS // 2
    out = np.empty((2, chunks, 2 * W, LAGS), ml_dtypes.bfloat16)
    for freq in range(2):
        sign = -1.0 if freq == 0 else 1.0
        for q in range(chunks):
            phase = bins_of(freq, q * W, W)[:, None] * shifts % length * (2.0 * math.pi / length)
            out[freq, q, :W] = (np.cos(phase) / math.sqrt(F)).astype(np.float32)
            out[freq, q, W:] = (sign * np.sin(phase) / math.sqrt(F)).astype(np.float32)
    return out


def dot(a, b):
    return jnp.dot(a, b, preferred_element_type=F32)


def iota(shape, dim):
    return lax.broadcasted_iota(jnp.int32, shape, dim)


def kernel(
    nz, ns, segs, chunks, slots, offs, traces, dead, cnt, four, delay, out,
    tr, crecv, inverse, table, dly, spec, power, own, recv, sel, mask, total, hoth, hrecv, fsend, frecv, vsum, srecv,
    tr_sem, c_send, c_recv, tab_sem, dly_sem, w_send, w_recv, h_send, h_recv, f_send, f_recv, s_send, s_recv,
):
    z = lax.axis_index("chan")
    s_me = lax.axis_index("seg")
    fq = lax.axis_index("freq")
    up = fq == 1
    half_len = table.shape[1]
    rows = own.shape[1]
    per = W // ns
    step = 2 * fq - 1
    dst = z + step
    src = z - step
    has_dst = jnp.logical_and(dst >= 0, dst < nz)
    has_src = jnp.logical_and(src >= 0, src < nz)
    twin = 1 - fq

    def table_copy(p):
        return pltpu.make_async_copy(four.at[fq, p], table.at[p], tab_sem.at[p])

    def trace_copy(s):
        return pltpu.make_async_copy(
            traces.at[pl.ds(s * W, W)], tr.at[pl.ds(s * W, W)], tr_sem.at[s]
        )

    table_copy(0).start()
    trace_copy(0).start()
    table_copy(1).start()
    for s in range(1, segs):
        trace_copy(s).start()
    for p in range(2, chunks + 1):
        table_copy(p).start()
    delay_copy = pltpu.make_async_copy(delay.at[fq], dly, dly_sem)
    delay_copy.start()

    sends_h = jnp.logical_and(up, z > 0)
    takes_h = z < nz - 1
    barrier = pltpu.get_barrier_semaphore()

    @pl.when(has_src)
    def _():
        pl.semaphore_signal(barrier, inc=1, device_id={"chan": src}, device_id_type=MESH)

    pl.semaphore_signal(barrier, inc=1, device_id={"freq": twin}, device_id_type=MESH)
    for d in range(1, ns):
        pl.semaphore_signal(
            barrier, inc=1, device_id={"seg": lax.rem(s_me + d, ns)}, device_id_type=MESH
        )

    @pl.when(takes_h)
    def _():
        for d in range(ns):
            giver = {"chan": z + 1, "seg": lax.rem(s_me + d, ns), "freq": 1}
            pl.semaphore_signal(barrier, inc=1, device_id=giver, device_id_type=MESH)

    diag = iota((W, W), 0) == iota((W, W), 1)
    cnt_col = jnp.sum(jnp.where(diag, cnt[...], 0).astype(F32), axis=1, keepdims=True)
    live_col = jnp.sum(jnp.where(diag, dead[...], 0).astype(F32), axis=1, keepdims=True)
    for s in range(segs):
        seg_number = (s_me * segs + s).astype(F32)
        valid = jnp.where(seg_number < cnt_col, live_col, 0.0)
        mask[s * W : (s + 1) * W, :] = jnp.broadcast_to(valid, (W, W))
    for k in range(slots):
        target = (iota((W, 2 * W), 0) - step * offs[k] + 2 * W) & (2 * W - 1)
        sel[k * W : (k + 1) * W, :] = jnp.where(iota((W, 2 * W), 1) == target, 1.0, 0.0).astype(BF16)

    @pl.when(jnp.logical_not(has_src))
    def _():
        def clear(q, carry):
            recv[q] = jnp.zeros((rows, 2 * W), BF16)
            return carry

        lax.fori_loop(0, chunks, clear, 0)
        crecv[...] = jnp.zeros_like(crecv)

    @pl.when(jnp.logical_not(takes_h))
    def _():
        hrecv[...] = jnp.zeros_like(hrecv)

    parity = (iota((1, 2 * W), 1) & 1).astype(F32)
    parity = (1.0 - 2.0 * parity) * (1 - 2 * fq).astype(F32)

    gap = iota((W, W), 0) - iota((W, W), 1)
    bands = [
        jnp.where(jnp.abs(gap + shift) <= HALF, 1.0, 0.0).astype(BF16) for shift in (-W, 0, W)
    ]

    def block(p, at):
        first = dot(tr[at, :half_len], table[p])
        second = dot(tr[at, half_len:], table[p])
        both = first + parity * second
        spec[p, at, :] = both
        square = both * both
        power[p + 1, at, :] = (square[:, :W] + square[:, W:]).astype(BF16)

    def whiten(q, at):
        window = (
            dot(power[q, at, :], bands[0]) + dot(power[q + 1, at, :], bands[1])
            + dot(power[q + 2, at, :], bands[2])
        )
        number = (jnp.minimum(q * W + iota((1, W), 1), HALF) + HALF + 1).astype(F32)
        factor = mask[at, :] * lax.rsqrt(window / number + EPS)
        own[q, at, :W] = (spec[q, at, :W] * factor).astype(BF16)
        own[q, at, W:] = (spec[q, at, W:] * factor).astype(BF16)

    def white_copy(q, at):
        return pltpu.make_async_remote_copy(
            src_ref=own.at[q, at], dst_ref=recv.at[q, at],
            send_sem=w_send.at[q], recv_sem=w_recv.at[q],
            device_id={"chan": dst}, device_id_type=MESH,
        )

    def send(q, at):
        @pl.when(has_dst)
        def _():
            white_copy(q, at).start()

    whole = pl.ds(0, rows)

    def rows_of(s):
        return pl.ds(pl.multiple_of(s * W, W), W)

    count_copy = pltpu.make_async_remote_copy(
        src_ref=cnt, dst_ref=crecv, send_sem=c_send, recv_sem=c_recv,
        device_id={"chan": dst}, device_id_type=MESH,
    )
    power[0] = jnp.zeros((rows, W), BF16)
    table_copy(0).wait()
    trace_copy(0).wait()
    block(0, rows_of(0))
    table_copy(1).wait()
    block(1, rows_of(0))
    whiten(0, rows_of(0))
    peers = ns + has_dst.astype(jnp.int32) + 2 * ns * sends_h.astype(jnp.int32)
    pl.semaphore_wait(barrier, peers)

    @pl.when(has_dst)
    def _():
        count_copy.start()

    send(0, rows_of(0))

    def first_chunk(s, carry):
        trace_copy(s).wait()
        block(0, rows_of(s))
        block(1, rows_of(s))
        whiten(0, rows_of(s))
        send(0, rows_of(s))
        return carry

    def early_chunk(p, s, carry):
        block(p, rows_of(s))
        whiten(p - 1, rows_of(s))
        send(p - 1, rows_of(s))
        return carry

    def later_chunk(p, carry):
        table_copy(p).wait()
        block(p, whole)
        whiten(p - 1, whole)
        send(p - 1, whole)
        return carry

    lax.fori_loop(1, segs, first_chunk, 0)
    for p in range(2, 4):
        table_copy(p).wait()
        lax.fori_loop(0, segs, functools.partial(early_chunk, p), 0)
    lax.fori_loop(4, chunks + 1, later_chunk, 0)
    delay_copy.wait()
    total[...] = jnp.zeros_like(total)

    @pl.when(has_src)
    def _():
        count_copy.wait_recv()

    counts = jnp.concatenate([cnt[...], crecv[...]], axis=1)
    for k in range(slots):
        target = (iota((W, 2 * W), 0) - step * offs[k] + 2 * W) & (2 * W - 1)
        partner = jnp.where(iota((W, 2 * W), 1) == target, counts, 0).astype(F32)
        fewer = jnp.minimum(cnt_col, jnp.sum(partner, axis=1, keepdims=True))
        inverse[k] = jnp.broadcast_to(1.0 / jnp.maximum(fewer, 1.0), (W, W))

    def correlate(q, carry):
        @pl.when(has_src)
        def _():
            white_copy(q, whole).wait_recv()

        re = [None] * slots
        im = [None] * slots
        for s in range(segs):
            at = slice(s * W, (s + 1) * W)
            mine = own[q, at, :]
            pair = dot(sel[...], jnp.concatenate([mine, recv[q, at, :]], axis=0))
            my_re = mine[:, :W].astype(F32)
            my_im = mine[:, W:].astype(F32)
            for k in range(slots):
                pair_re = pair[k * W : (k + 1) * W, :W]
                pair_im = pair[k * W : (k + 1) * W, W:]
                one = my_re * pair_re + my_im * pair_im
                two = my_im * pair_re - my_re * pair_im
                re[k] = one if s == 0 else re[k] + one
                im[k] = two if s == 0 else im[k] + two
        for k in range(slots):
            scale = inverse[k]
            cross = jnp.concatenate([re[k] * scale, im[k] * scale], axis=1).astype(BF16)
            total[k] += dot(cross, dly[q])
        return carry

    lax.fori_loop(0, chunks, correlate, 0)

    gap = iota((W, W), 1) - iota((W, W), 0)
    half = LAGS // 2

    def h_copy(d, q):
        peer = lax.rem(s_me + d, ns)
        return pltpu.make_async_remote_copy(
            src_ref=hoth.at[:, pl.ds(pl.multiple_of(peer * per, per), per), q * half : (q + 1) * half],
            dst_ref=hrecv.at[d], send_sem=h_send.at[d, q], recv_sem=h_recv.at[d],
            device_id={"chan": z - 1, "seg": peer, "freq": q}, device_id_type=MESH,
        )

    f_copy = pltpu.make_async_remote_copy(
        src_ref=fsend, dst_ref=frecv, send_sem=f_send, recv_sem=f_recv,
        device_id={"freq": twin}, device_id_type=MESH,
    )

    def s_copy(d):
        peer = lax.rem(s_me + d, ns)
        return pltpu.make_async_remote_copy(
            src_ref=vsum.at[:, pl.ds(pl.multiple_of(peer * per, per), per)],
            dst_ref=srecv.at[d - 1], send_sem=s_send.at[d - 1], recv_sem=s_recv.at[d - 1],
            device_id={"seg": peer}, device_id_type=MESH,
        )

    @pl.when(up)
    def _():
        for k in range(slots):
            moved = dot(jnp.where(gap == offs[k] - W, 1.0, 0.0).astype(BF16), total[k].astype(BF16))
            hoth[k] = moved.astype(BF16)

        @pl.when(sends_h)
        def _():
            for d in reversed(range(ns)):
                for q in range(2):
                    h_copy(d, q).start()

        for k in range(slots):
            total[k] = dot(jnp.where(gap == offs[k], 1.0, 0.0).astype(BF16), total[k].astype(BF16))

    kept = pl.ds(pl.multiple_of(fq * half, half), half)
    given = pl.ds(pl.multiple_of(twin * half, half), half)
    for k in range(slots):
        fsend[k] = total[k, :, given].astype(BF16)
    f_copy.start()
    f_copy.wait_recv()
    for k in range(slots):
        merged = total[k, :, kept] + frecv[k].astype(F32)
        total[k, :, kept] = merged
        vsum[k] = merged.astype(BF16)
    for d in range(1, ns):
        s_copy(d).start()
    for d in range(1, ns):
        s_copy(d).wait_recv()

    @pl.when(takes_h)
    def _():
        for d in range(ns):
            h_copy(d, 0).wait_recv()

    for k in range(slots):
        result = total[k, pl.ds(pl.multiple_of(s_me * per, per), per), kept]
        for d in range(1, ns):
            result += srecv[d - 1, k].astype(F32)
        for d in range(ns):
            result += hrecv[d, k].astype(F32)
        out[k] = result

    @pl.when(has_dst)
    def _():
        def drain(q, carry):
            white_copy(q, whole).wait_send()
            return carry

        lax.fori_loop(0, chunks, drain, 0)
        count_copy.wait_send()

    @pl.when(sends_h)
    def _():
        for d in range(ns):
            for q in range(2):
                h_copy(d, q).wait_send()

    f_copy.wait_send()
    for d in range(1, ns):
        s_copy(d).wait_send()


def shards(traces, dead_mask, seg_counts, offsets):
    segs, chans, length = traces.shape
    nz, ns = lax.axis_size("chan"), lax.axis_size("seg")
    slots = offsets.shape[0]
    chunks = F // 2 // W
    rows = segs * chans
    per = chans // ns
    half = LAGS // 2
    vmem = pl.BlockSpec(memory_space=pltpu.VMEM)
    hbm = pl.BlockSpec(memory_space=pl.ANY)
    dma = pltpu.SemaphoreType.DMA
    terms = pl.pallas_call(
        functools.partial(kernel, nz, ns, segs, chunks, slots),
        out_shape=jax.ShapeDtypeStruct((slots, per, half), F32),
        in_specs=[pl.BlockSpec(memory_space=pltpu.SMEM), hbm, vmem, vmem, hbm, hbm],
        out_specs=vmem,
        scratch_shapes=[
            pltpu.VMEM((rows, length), BF16),
            pltpu.VMEM((1, chans), jnp.int32),
            pltpu.VMEM((slots, W, W), F32),
            pltpu.VMEM((chunks + 1, length // 2, 2 * W), BF16),
            pltpu.VMEM((chunks, 2 * W, LAGS), BF16),
            pltpu.VMEM((chunks + 1, rows, 2 * W), F32),
            pltpu.VMEM((chunks + 2, rows, W), BF16),
            pltpu.VMEM((chunks, rows, 2 * W), BF16),
            pltpu.VMEM((chunks, rows, 2 * W), BF16),
            pltpu.VMEM((slots * W, 2 * W), BF16),
            pltpu.VMEM((rows, W), F32),
            pltpu.VMEM((slots, W, LAGS), F32),
            pltpu.VMEM((slots, W, LAGS), BF16),
            pltpu.VMEM((ns, slots, per, half), BF16),
            pltpu.VMEM((slots, W, half), BF16),
            pltpu.VMEM((slots, W, half), BF16),
            pltpu.VMEM((slots, W, half), BF16),
            pltpu.VMEM((max(ns - 1, 1), slots, per, half), BF16),
            dma((segs,)),
            dma,
            dma,
            dma((chunks + 1,)),
            dma,
            dma((chunks,)),
            dma((chunks,)),
            dma((ns, 2)),
            dma((ns,)),
            dma,
            dma,
            dma((max(ns - 1, 1),)),
            dma((max(ns - 1, 1),)),
        ],
        compiler_params=pltpu.CompilerParams(
            collective_id=0, has_side_effects=True, vmem_limit_bytes=56 * 1024 * 1024
        ),
    )(
        offsets,
        traces.reshape(rows, length),
        dead_mask.reshape(1, chans),
        seg_counts.reshape(1, chans),
        jnp.asarray(fourier_blocks(length, chunks)),
        jnp.asarray(delay_blocks(length, chunks)),
    )
    return jnp.transpose(terms, (1, 0, 2))


def solution(mesh):
    in_specs = (
        P("seg", ("groups", "chan"), None),
        P(("groups", "chan")),
        P(("groups", "chan")),
        P(),
    )
    out_specs = P(("groups", "chan", "seg"), None, "freq")
    return jax.shard_map(shards, mesh=mesh, in_specs=in_specs, out_specs=out_specs, check_vma=False)
```
